512 devices in a mesh: row: 32 (over z, core), col: 16 (over x, y).
Axes of the slice: x: 4, y: 4, z: 16, core: 2. Of those that a mesh axis runs over, the one named last changes fastest.
Arguments:
- source: bfloat16 [32768, 256], P(('row', 'col')), may hold values from -1.5 to 1.5
- target: bfloat16 [32768, 256], P(('col', 'row')), may hold values from -1.5 to 1.5
- g_init: float32 [32768], P('col'), may hold values from -25 to 25
- pairs: int32 [64, 64], P('row', 'col'), may hold values from 0 to 1, as said below
Outputs:
- f_out: float32 [32768], P('row')
- g_out: float32 [32768], P('col')
The draws below stay inside these ranges and needn't reach their ends.
Inputs may be any that keep to these rules, and one draw needn't show every extreme that they name: Values are 0 or 1; every block of source cells and every block of target cells has at least one kept pair; the share of kept pairs differs between devices' tiles.
All inputs are finite; a program needn't handle non-finite values.
Results may differ from the reference program's by a relative error of at most 0.0003.
Values may be sent and summed in bfloat16 or wider, within the bound.
No kernel may reach another device: no remote copies, remote signals or barrier semaphores. Data moves between devices by JAX's collectives and lax.ppermute only.
A program may use at most 64 MiB of HBM per device.

```python
import jax
import jax.numpy as jnp
from jax import lax

DL = 256
BLK = 512
ROWS_DEV = 1024
COLS_DEV = 2048
NS = 32768
NT = 32768
NBR = 64
NBC = 64


cell_types = 8


trajectory_rank = 4


outlier_scale = 8.0


def atlas_cells(key, count, salt):
    shared = jax.random.fold_in(key, 7)
    centre_key, basis_key = jax.random.split(shared)
    root = jnp.sqrt(jnp.float32(DL))
    centres = 1.2247 * jax.random.normal(centre_key, (cell_types, DL), jnp.float32) / root
    basis = jax.random.normal(basis_key, (cell_types * trajectory_rank, DL), jnp.float32) / root
    own = jax.random.fold_in(key, salt)
    kind_key, place_key, noise_key, scale_key, odd_key, forced_key = jax.random.split(own, 6)
    kinds = jax.random.randint(kind_key, (count,), 0, cell_types)
    onehot = (kinds[:, None] == jnp.arange(cell_types, dtype=jnp.int32)[None, :]).astype(jnp.float32)
    place = 0.6 * jax.random.normal(place_key, (count, trajectory_rank), jnp.float32)
    mixing = (onehot[:, :, None] * place[:, None, :]).reshape(count, cell_types * trajectory_rank)
    noise = jax.random.normal(noise_key, (count, DL), jnp.float32) / root
    spread = jnp.exp(jax.random.uniform(scale_key, (count, 1), jnp.float32, jnp.log(jnp.float32(0.5)), jnp.log(jnp.float32(1.5))))
    forced = jax.random.randint(forced_key, (), 0, count)
    outlier = (jax.random.randint(odd_key, (count,), 0, 32) == 0) | (jnp.arange(count, dtype=jnp.int32) == forced)
    spread = jnp.where(outlier[:, None], jnp.float32(outlier_scale), spread)
    centre_part = jnp.dot(onehot, centres, precision=jax.lax.Precision.HIGHEST)
    trajectory = jnp.dot(mixing, basis, precision=jax.lax.Precision.HIGHEST)
    return jnp.clip(centre_part + trajectory + spread * noise, -1.5, 1.5)


def draw_source(key, part):
    return atlas_cells(key, NS, 21).astype(jnp.bfloat16)


def draw_target(key, part):
    return atlas_cells(key, NT, 22).astype(jnp.bfloat16)


def draw_g_init(key, part):
    first, second, third, fourth = jax.random.split(key, 4)
    marked = jax.random.randint(second, (NBC,), 0, 8) == 0
    chosen = jax.random.randint(fourth, (), 0, NBC)
    marked = marked | (jnp.arange(NBC, dtype=jnp.int32) == chosen)
    lift = jnp.repeat(marked, BLK).astype(jnp.float32)
    jitter = jax.random.uniform(third, (NT,), jnp.float32, 0.0, 0.3)
    base = jnp.clip(0.3 * jax.random.normal(first, (NT,), jnp.float32), -1.5, 1.5)
    return base + lift * (20.0 + jitter)


def draw_pairs(key, part):
    first, second, third, fourth = jax.random.split(key, 4)
    rows_index = jnp.arange(NBR, dtype=jnp.int32)
    cols_index = jnp.arange(NBC, dtype=jnp.int32)
    col_pick = jax.random.permutation(first, NBC)
    row_pick = jax.random.permutation(second, NBR)
    base = (cols_index[None, :] == col_pick[rows_index % NBC][:, None]) | (rows_index[:, None] == row_pick[cols_index % NBR][None, :])
    row_tile = ROWS_DEV // BLK
    col_tile = COLS_DEV // BLK
    levels = jax.random.randint(third, (NBR // row_tile, NBC // col_tile), 1, 20)
    level = levels[(rows_index // row_tile)[:, None], (cols_index // col_tile)[None, :]]
    drawn = jax.random.randint(fourth, (NBR, NBC), 0, 32) < level
    return (base | drawn).astype(jnp.int32)


def setup_inputs(seed: int = 0) -> dict:
    splits = jax.random.split(jax.random.key(seed), 5)
    source = draw_source(jax.random.fold_in(splits[4], 71), 0)
    target = draw_target(jax.random.fold_in(splits[4], 71), 0)
    g_init = draw_g_init(jax.random.fold_in(splits[4], 71), 0)
    pairs = draw_pairs(jax.random.fold_in(splits[4], 71), 0)
    return dict(source=source, target=target, g_init=g_init, pairs=pairs)


EPSILON = 0.1
VERY_LOW = -1e30


def block_cost(rows, cols):
    inner = lax.dot_general(rows, cols, (((1,), (1,)), ((), ())), preferred_element_type=jnp.float32)
    left = 0.5 * jnp.sum(jnp.square(rows.astype(jnp.float32)), axis=1)
    right = 0.5 * jnp.sum(jnp.square(cols.astype(jnp.float32)), axis=1)
    return left[:, None] + right[None, :] - inner


def reference(source, target, g_init, pairs):
    log_nt = jnp.log(jnp.float32(NT))
    log_ns = jnp.log(jnp.float32(NS))

    def row_part(index):
        rows = lax.dynamic_slice_in_dim(source, index * BLK, BLK, 0)
        keep = jnp.repeat(lax.dynamic_index_in_dim(pairs, index, 0, keepdims=False) > 0, BLK)
        score = (g_init[None, :] - block_cost(rows, target)) / EPSILON - log_nt
        peak = jnp.max(jnp.where(keep[None, :], score, VERY_LOW), axis=1)
        total = jnp.sum(jnp.where(keep[None, :], jnp.exp(score - peak[:, None]), 0.0), axis=1)
        return -EPSILON * (peak + jnp.log(total))

    f_out = lax.map(row_part, jnp.arange(NBR, dtype=jnp.int32)).reshape(NS)

    def col_step(carry, index):
        peak, total = carry
        rows = lax.dynamic_slice_in_dim(source, index * BLK, BLK, 0)
        values = lax.dynamic_slice_in_dim(f_out, index * BLK, BLK, 0)
        keep = jnp.repeat(lax.dynamic_index_in_dim(pairs, index, 0, keepdims=False) > 0, BLK)
        score = (values[:, None] - block_cost(rows, target)) / EPSILON - log_ns
        block_peak = jnp.max(jnp.where(keep[None, :], score, VERY_LOW), axis=0)
        new_peak = jnp.maximum(peak, block_peak)
        added = jnp.sum(jnp.where(keep[None, :], jnp.exp(score - new_peak[None, :]), 0.0), axis=0)
        total = total * jnp.exp(peak - new_peak) + added
        return (new_peak, total), None

    start = (jnp.full((NT,), VERY_LOW, jnp.float32), jnp.zeros((NT,), jnp.float32))
    (peak, total), _ = lax.scan(col_step, start, jnp.arange(NBR, dtype=jnp.int32))
    g_out = -EPSILON * (peak + jnp.log(total))
    return f_out, g_out
```

```python
import math

import jax
import jax.numpy as jnp
from jax import lax
from jax.experimental import pallas as pl
from jax.experimental.pallas import tpu as pltpu
from jax.sharding import Mesh
from jax.sharding import PartitionSpec as P


BLK = 512
DL = 256
LANES = 128
EPSILON = 0.1
VERY_LOW = -1e30
SCALE = math.log2(math.e) / EPSILON
UNSCALE = EPSILON * math.log(2.0)
ROW = ("z", "core")
VMEM = pl.BlockSpec(memory_space=pltpu.VMEM)
SMEM = pl.BlockSpec(memory_space=pltpu.SMEM)
f32 = jnp.float32


def half_norms(x):
    x = x.astype(f32)
    return 0.5 * jnp.sum(x * x, axis=1, keepdims=True)


def turned(x):
    rows = x.shape[0]
    if rows < LANES:
        x = jnp.concatenate([x, jnp.zeros((LANES - rows, LANES), f32)], axis=0)
    return x.T


def joined(parts):
    peak = jnp.max(parts, axis=0)
    return peak + jnp.log2(jnp.sum(jnp.exp2(parts - peak[None]), axis=0))


def reduced_over(kept, many, few, left, right, bias_ref, score_ref, peak_ref, total_ref):
    peak_ref[...] = jnp.full(peak_ref.shape, VERY_LOW, f32)
    total_ref[...] = jnp.zeros(total_ref.shape, f32)
    per = BLK // LANES

    def scores(step, _):
        a, b = step // few, step % few

        @pl.when(kept(a, b))
        def _():
            y = right(b)
            peak = peak_ref[b]
            for q in range(per):
                x = left(a * per + q)
                inner = lax.dot_general(
                    x, y, (((1,), (1,)), ((), ())), preferred_element_type=f32
                )
                bias = bias_ref[a * per + q]
                s = inner * SCALE + jnp.concatenate([bias] * (BLK // LANES), axis=1)
                score_ref[step, q] = s
                peak = jnp.maximum(peak, jnp.max(s.reshape(LANES // 8, 8, BLK), axis=0))
            peak_ref[b] = peak

        return 0

    def sums(step, _):
        a, b = step // few, step % few

        @pl.when(kept(a, b))
        def _():
            peak = peak_ref[b]
            total = total_ref[b]
            for q in range(per):
                s = score_ref[step, q].reshape(LANES // 8, 8, BLK)
                total = total + jnp.sum(jnp.exp2(s - peak[None]), axis=0)
            total_ref[b] = total

        return 0

    lax.fori_loop(0, many * few, scores, 0)
    lax.fori_loop(0, many * few, sums, 0)
    lines = []
    for b in range(few):
        peak, total = peak_ref[b], total_ref[b]
        top = jnp.max(peak, axis=0, keepdims=True)
        total = jnp.sum(total * jnp.exp2(peak - top), axis=0, keepdims=True)
        line = jnp.where(total > 0.0, top + jnp.log2(total), VERY_LOW)
        lines += [line[:, k * LANES : (k + 1) * LANES] for k in range(per)]
    return lines


def row_kernel(pairs_ref, core_ref, src_ref, own_ref, other_ref, g_ref,
               out_ref, tgt_ref, right_ref,
               line_ref, bias_ref, score_ref, peak_ref, total_ref):
    core = core_ref[0]
    tgt_ref[:, core] = own_ref[...]
    tgt_ref[:, 1 - core] = other_ref[...]
    lines = tgt_ref.shape[0]
    g = turned(g_ref[...])
    lane = lax.broadcasted_iota(jnp.int32, (LANES, LANES), 1)
    norms = jnp.zeros((LANES, LANES), f32)
    for k in range(lines):
        n = half_norms(tgt_ref[k].reshape(LANES, DL))
        norms = jnp.where(lane == k, n, norms)
        bias_ref[k] = jnp.broadcast_to((g[:, k : k + 1] - n) * SCALE, (LANES, LANES))
    right_ref[...] = norms.T[:lines]
    found = reduced_over(
        lambda a, b: pairs_ref[b, a] > 0,
        4, 2,
        lambda k: tgt_ref[k].reshape(LANES, DL),
        lambda b: src_ref[pl.ds(b * 8, 8)].reshape(BLK, DL),
        bias_ref, score_ref, peak_ref, total_ref,
    )
    for k, line in enumerate(found):
        line_ref[k : k + 1] = line
    out_ref[...] = jnp.broadcast_to(line_ref[...][None], out_ref.shape)


def col_kernel(log2_nt, log2_ns, pairs_ref, src_ref, tgt_ref, got_ref,
               out_ref, f_ref,
               bias_ref, score_ref, peak_ref, total_ref):
    u = joined(got_ref[...])
    lines = u.shape[0]
    ut = turned(u)
    lane = lax.broadcasted_iota(jnp.int32, (LANES, LANES), 1)
    norms = jnp.zeros((LANES, LANES), f32)
    for k in range(lines):
        n = half_norms(src_ref[2 * k : 2 * k + 2].reshape(LANES, DL))
        norms = jnp.where(lane == k, n, norms)
        bias_ref[k] = jnp.broadcast_to((log2_nt - log2_ns) - ut[:, k : k + 1], (LANES, LANES))
    f_ref[...] = norms.T[:lines] + UNSCALE * (log2_nt - u)
    found = reduced_over(
        lambda a, b: pairs_ref[a, b] > 0,
        2, 4,
        lambda k: src_ref[pl.ds(2 * k, 2)].reshape(LANES, DL),
        lambda b: tgt_ref[pl.ds(b * 4, 4)].reshape(BLK, DL),
        bias_ref, score_ref, peak_ref, total_ref,
    )
    for k, line in enumerate(found):
        out_ref[k : k + 1] = line


def spread_kernel(got_ref, out_ref):
    out_ref[...] = jnp.broadcast_to(joined(got_ref[...])[None], out_ref.shape)


def last_kernel(got_ref, right_ref, g_ref):
    g_ref[...] = right_ref[...] - UNSCALE * joined(got_ref[...])


def shape(*dims, dtype=f32):
    return jax.ShapeDtypeStruct(dims, dtype)


def local(source, target, g_init, pairs):
    cols, zs = lax.axis_size("col"), lax.axis_size("z")
    sources = lax.all_to_all(
        jnp.broadcast_to(source[None], (cols, *source.shape)), "col", 0, 0, tiled=True
    )
    own = lax.all_gather(target, "z")
    other = lax.ppermute(own, "core", [(0, 1), (1, 0)])
    core = lax.axis_index("core").astype(jnp.int32).reshape(1)
    rows_dev = sources.shape[0] * sources.shape[1]
    cols_dev = 2 * own.shape[0] * own.shape[1]
    log2_nt = math.log2(cols * cols_dev)
    log2_ns = math.log2(zs * 2 * rows_dev)
    rl, cl = rows_dev // LANES, cols_dev // LANES
    rb, cb = pairs.shape
    scratch = lambda few, lines: [
        pltpu.VMEM((lines, LANES, LANES), f32),
        pltpu.VMEM((rb * cb, BLK // LANES, LANES, BLK), f32),
        pltpu.VMEM((few, 8, BLK), f32),
        pltpu.VMEM((few, 8, BLK), f32),
    ]
    spread, targets, right = pl.pallas_call(
        row_kernel,
        out_shape=(shape(cols, rl, LANES), shape(zs, 2, *target.shape, dtype=target.dtype), shape(cl, LANES)),
        in_specs=[SMEM, SMEM, VMEM, VMEM, VMEM, VMEM],
        out_specs=(VMEM, VMEM, VMEM),
        scratch_shapes=[pltpu.VMEM((rl, LANES), f32)] + scratch(rb, cl),
        compiler_params=pltpu.CompilerParams(vmem_limit_bytes=24 << 20),
        name="row_pass",
    )(pairs, core, sources, own, other, g_init.reshape(cl, LANES))
    got = lax.all_to_all(spread, "col", 0, 0, tiled=True)
    partial, f = pl.pallas_call(
        lambda *refs: col_kernel(log2_nt, log2_ns, *refs),
        out_shape=(shape(cl, LANES), shape(rl, LANES)),
        in_specs=[SMEM, VMEM, VMEM, VMEM],
        out_specs=(VMEM, VMEM),
        scratch_shapes=scratch(cb, rl),
        compiler_params=pltpu.CompilerParams(vmem_limit_bytes=24 << 20),
        name="col_pass",
    )(pairs, sources, targets, got)
    both = lax.all_gather(partial, "core")
    spread = pl.pallas_call(
        spread_kernel,
        out_shape=shape(zs, cl, LANES),
        in_specs=[VMEM],
        out_specs=VMEM,
        compiler_params=pltpu.CompilerParams(vmem_limit_bytes=4 << 20),
        name="spread",
    )(both)
    got = lax.all_to_all(spread, "z", 0, 0, tiled=True)
    g = pl.pallas_call(
        last_kernel,
        out_shape=shape(cl, LANES),
        in_specs=[VMEM, VMEM],
        out_specs=VMEM,
        compiler_params=pltpu.CompilerParams(vmem_limit_bytes=4 << 20),
        name="last",
    )(got, right)
    return (f.reshape(rows_dev), g.reshape(cols_dev))


def solution(mesh):
    finer = Mesh(mesh.devices.reshape(-1, 2, mesh.shape["col"]), ("z", "core", "col"))
    placed = (P(("z", "core", "col"), None), P(("col", "z", "core"), None), P("col"), P(ROW, "col"))
    return jax.shard_map(
        local, mesh=finer, in_specs=placed, out_specs=(P(ROW), P("col")), check_vma=False
    )
```

```python
import math

import jax
import jax.numpy as jnp
from jax import lax
from jax.experimental import pallas as pl
from jax.experimental.pallas import tpu as pltpu
from jax.sharding import Mesh
from jax.sharding import PartitionSpec as P


BLK = 512
DL = 256
LANES = 128
SUB = 8
EPSILON = 0.1
VERY_LOW = -1e30
SCALE = 1.0 / EPSILON
ROW = ("z", "core")
VMEM = pl.BlockSpec(memory_space=pltpu.VMEM)
SMEM = pl.BlockSpec(memory_space=pltpu.SMEM)
f32 = jnp.float32


def half_norms(x):
    x = x.astype(f32)
    return 0.5 * jnp.sum(x * x, axis=1, keepdims=True)


def dot(x, y):
    return lax.dot_general(x, y, (((1,), (1,)), ((), ())), preferred_element_type=f32)


def turned(x):
    rows = x.shape[0]
    if rows < LANES:
        x = jnp.concatenate([x, jnp.zeros((LANES - rows, LANES), f32)], axis=0)
    return x.T


def wide(x, times):
    return jnp.concatenate([x] * times, axis=1)


def joined(parts):
    peak = jnp.max(parts, axis=0)
    return peak + jnp.log(jnp.sum(jnp.exp(parts - peak[None]), axis=0))


def added(state, s):
    s = s.reshape(s.shape[0] // SUB, SUB, s.shape[1])
    peak = jnp.max(s, axis=0)
    if state is not None:
        peak = jnp.maximum(peak, state[0])
    total = jnp.sum(jnp.exp(s - peak[None]), axis=0)
    if state is not None:
        total = total + state[1] * jnp.exp(state[0] - peak)
    return peak, total


def closed(peak, total):
    top = jnp.max(peak, axis=0, keepdims=True)
    total = jnp.sum(total * jnp.exp(peak - top), axis=0, keepdims=True)
    return jnp.where(top > 0.5 * VERY_LOW, top + jnp.log(total), VERY_LOW)


def fan_kernel(x_ref, out_ref):
    out_ref[...] = jnp.broadcast_to(x_ref[...][None], out_ref.shape)


def keep_bias(pairs_ref, rb, cb):
    return jnp.where(pairs_ref[rb, cb] > 0, 0.0, VERY_LOW)


def piece_kernel(index, *refs):
    last = index == 1
    pairs_ref, place_ref, q_ref, g_ref, src_ref = refs[:5]
    if last:
        peak_in, total_in, _, norm_in, out_ref, right_ref, tgt_ref, bias_ref, turn_ref, line_ref = refs[5:]
    else:
        peak_ref, total_ref, tgt_ref, norm_ref, bias_ref, turn_ref = refs[5:]
    place = place_ref[0]
    group = (place + place // 2 + index) % 2
    chips = q_ref.shape[0]
    lane = lax.broadcasted_iota(jnp.int32, (64, LANES), 1)
    norms = jnp.zeros((64, LANES), f32)
    turn_ref[...] = turned(g_ref[...])
    for z in range(chips):
        core = (group + z) % 2
        g = turn_ref[pl.ds(pl.multiple_of(core * 64, 64), 64), :]
        x = q_ref[z]
        tgt_ref[z, core] = x
        n = half_norms(x)
        norms = jnp.where(lane == z, n, norms)
        bias_ref[z] = jnp.broadcast_to((g[:, z : z + 1] - n) * SCALE, (64, LANES))
    per = 2
    lines = []
    for rb in range(pairs_ref.shape[0]):
        y = src_ref[rb * 8 : rb * 8 + 8].reshape(BLK, DL)
        state = (peak_in[rb], total_in[rb]) if last else None
        for c in range(0, chips, per):
            x = q_ref[c : c + per].reshape(per * 64, DL)
            bias = bias_ref[c : c + per].reshape(per * 64, LANES) + keep_bias(pairs_ref, rb, c // 4)
            state = added(state, dot(x, y) * SCALE + wide(bias, BLK // LANES))
        if last:
            line = closed(*state)
            lines += [line[:, k * LANES : (k + 1) * LANES] for k in range(BLK // LANES)]
        else:
            peak_ref[rb], total_ref[rb] = state
    if last:
        for k, line in enumerate(lines):
            line_ref[k : k + 1] = line
        out_ref[...] = jnp.broadcast_to(line_ref[...][None], out_ref.shape)
        swapped = (lane + group) % 2 == 0
        first, second = jnp.where(swapped, norms, norm_in[...]), jnp.where(swapped, norm_in[...], norms)
        right_ref[...] = jnp.concatenate([first, second], axis=0).T[:chips]
    else:
        norm_ref[...] = norms


def col_kernel(log_nt, log_ns, pairs_ref, src_ref, tgt_ref, got_ref, out_ref, f_ref, bias_ref):
    u = joined(got_ref[...])
    lines = u.shape[0]
    ut = turned((log_nt - log_ns) - u)
    lane = lax.broadcasted_iota(jnp.int32, (LANES, LANES), 1)
    norms = jnp.zeros((LANES, LANES), f32)
    for k in range(lines):
        n = half_norms(src_ref[2 * k : 2 * k + 2].reshape(LANES, DL))
        norms = jnp.where(lane == k, n, norms)
        bias_ref[k] = jnp.broadcast_to(ut[:, k : k + 1], (LANES, LANES))
    f_ref[...] = norms.T[:lines] + EPSILON * (log_nt - u)
    _, cbs = pairs_ref.shape
    for b in range(cbs):
        y = tgt_ref[b * 4 : b * 4 + 4].reshape(BLK, DL)
        state = None
        for k in range(lines):
            x = src_ref[2 * k : 2 * k + 2].reshape(LANES, DL)
            bias = bias_ref[k] + keep_bias(pairs_ref, k * LANES // BLK, b)
            state = added(state, dot(x, y) * SCALE + wide(bias, BLK // LANES))
        line = closed(*state)
        for k in range(BLK // LANES):
            out_ref[4 * b + k : 4 * b + k + 1] = line[:, k * LANES : (k + 1) * LANES]


def spread_kernel(got_ref, out_ref):
    out_ref[...] = jnp.broadcast_to(joined(got_ref[...])[None], out_ref.shape)


def last_kernel(got_ref, right_ref, g_ref):
    g_ref[...] = right_ref[...] - EPSILON * joined(got_ref[...])


def shape(*dims, dtype=f32):
    return jax.ShapeDtypeStruct(dims, dtype)


def kernel_call(body, outs, ins, mib=8, scratch=(), aliases={}, flops=0, bytes_accessed=0):
    single = not isinstance(outs, tuple)
    return pl.pallas_call(
        body,
        out_shape=outs,
        in_specs=ins,
        out_specs=VMEM if single else (VMEM,) * len(outs),
        scratch_shapes=list(scratch),
        input_output_aliases=aliases,
        compiler_params=pltpu.CompilerParams(vmem_limit_bytes=mib << 20),
        cost_estimate=pl.CostEstimate(flops=flops, bytes_accessed=bytes_accessed, transcendentals=0),
    )


def local(source, target, g_init, pairs):
    cols, zs = lax.axis_size("col"), lax.axis_size("z")
    rows_dev, cols_dev = cols * source.shape[0], 2 * zs * target.shape[0]
    log_nt, log_ns = math.log(cols * cols_dev), math.log(zs * 2 * rows_dev)
    rl, cl = rows_dev // LANES, cols_dev // LANES
    rb, _ = pairs.shape
    alternating = [[2 * z + (z + group) % 2 for z in range(zs)] for group in range(2)]

    fanned = kernel_call(fan_kernel, shape(cols, *source.shape, dtype=source.dtype), [VMEM], mib=2)(source)
    sources = lax.all_to_all(fanned, "col", 0, 0, tiled=True)
    g_lines = g_init.reshape(cl, LANES)
    near = lax.all_gather(target, ROW, axis_index_groups=alternating)
    other = lax.ppermute(near, "core", [(0, 1), (1, 0)])
    place = lax.axis_index(ROW).astype(jnp.int32).reshape(1)

    kept = shape(zs, 2, *target.shape, dtype=target.dtype)
    bias = [pltpu.VMEM((zs, 64, LANES), f32), pltpu.VMEM((LANES, LANES), f32)]
    state = (shape(rb, SUB, BLK),) * 2
    work = dict(flops=cols_dev * rows_dev * DL, bytes_accessed=1 << 20)
    state = kernel_call(
        lambda *refs: piece_kernel(0, *refs),
        (*state, kept, shape(64, LANES)),
        [SMEM, SMEM, VMEM, VMEM, VMEM], scratch=bias, **work,
    )(pairs, place, near, g_lines, sources)
    sent, right, targets = kernel_call(
        lambda *refs: piece_kernel(1, *refs),
        (shape(cols, rl, LANES), shape(cl, LANES), kept),
        [SMEM, SMEM] + [VMEM] * 7, scratch=[*bias, pltpu.VMEM((rl, LANES), f32)], aliases={7: 2}, **work,
    )(pairs, place, other, g_lines, sources, *state)
    got = lax.all_to_all(sent, "col", 0, 0, tiled=True)
    partial, f = kernel_call(
        lambda *refs: col_kernel(log_nt, log_ns, *refs),
        (shape(cl, LANES), shape(rl, LANES)),
        [SMEM, VMEM, VMEM, VMEM], scratch=[pltpu.VMEM((rl, LANES, LANES), f32)],
    )(pairs, sources, targets, got)
    both = lax.all_gather(partial, "core")
    sent = kernel_call(spread_kernel, shape(zs, cl, LANES), [VMEM], mib=4)(both)
    got = lax.all_to_all(sent, "z", 0, 0, tiled=True)
    g = kernel_call(last_kernel, shape(cl, LANES), [VMEM, VMEM], mib=4)(got, right)
    return (f.reshape(rows_dev), g.reshape(cols_dev))


def solution(mesh):
    finer = Mesh(mesh.devices.reshape(-1, 2, mesh.shape["col"]), (*ROW, "col"))
    placed = (P((*ROW, "col"), None), P(("col", *ROW), None), P("col"), P(ROW, "col"))
    return jax.shard_map(local, mesh=finer, in_specs=placed, out_specs=(P(ROW), P("col")), check_vma=False)
```
